1024 devices in a mesh: group: 4 (over z_hi), dp: 4 (over z_lo), mp: 64 (over y, x, core).
Axes of the slice: x: 4, y: 8, z: 16 (z_hi: 4, z_lo: 4; z = z_hi * 4 + z_lo), core: 2. Of those that a mesh axis runs over, the one named last changes fastest.
Arguments:
- patch_rows: bfloat16 [16, 128, 1280], P(('group', 'dp')), may hold values from -6 to 6
- ln_gain: float32 [1280], replicated, may hold values from 0.5 to 1.5
- ln_bias: float32 [1280], replicated, may hold values from -1.5 to 1.5
- merge_up: bfloat16 [5120, 5120], P(None, 'mp'), may hold values from -0.078125 to 0.078125
- merge_up_bias: float32 [5120], P('mp'), may hold values from -2.5 to 2.5
- merge_down: bfloat16 [5120, 8192], P('mp'), may hold values from -0.078125 to 0.078125
- merge_down_bias: float32 [8192], P('mp'), may hold values from -2.5 to 2.5
- row_owner: int32 [512, 1], replicated, may hold values from 0 to 15; in each aligned block of 32 rows (0 to 31, 32 to 63, ...) at most 4 rows name the same one
- text_embed: bfloat16 [16, 256, 8192], P(('group', 'dp')), may hold values from -6 to 6
- doc_ids: int32 [16, 256], P(('group', 'dp')), may hold values from 0 to 7, never falling along the last dimension, each value on 1 to 64 neighbouring positions
- rms_gain: float32 [8192], replicated, may hold values from 0.5 to 1.5
- w_query: bfloat16 [8192, 8192], P(None, 'mp'), as said below
- query_bias: float32 [8192], P('mp'), may hold values from -2.5 to 2.5
- w_keyval: bfloat16 [8192, 2, 1024], P(None, None, 'mp'), may hold values from -0.0625 to 0.0625
- keyval_bias: float32 [2, 1024], P(None, 'mp'), may hold values from -2.5 to 2.5
Outputs:
- attention: bfloat16 [16, 256, 8192], P(('group', 'dp'), None, 'mp')
The draws below stay inside these ranges and needn't reach their ends.
Inputs may be any that keep to these rules, and one draw needn't show every extreme that they name: `row_owner`: in each aligned block of 32 rows (the rows of one image owner) no owner is named more than 4 times, a bound that some block reaches. `w_query`: columns are independent with entries of scale about D ** -0.5 or larger.
All inputs are finite; a program needn't handle non-finite values.
Results may differ from the reference program's by a relative error of at most 0.014.
The reference program's roundings to bfloat16 on the way count: a program that leaves them out, or rounds other values in their place, can miss the bound.
Values may be sent and summed in bfloat16 or wider, within the bound.
A program may use at most 64 MiB of HBM per device.

```python
import math
import jax
import jax.numpy as jnp
import numpy as np
from jax import lax

D = 8192
HEADS = 64
KV_HEADS = 8
HEAD_DIM = 128
VIS_WIDTH = 1280
MERGE_HIDDEN = 5120
M_DEV = 32
S_DEV = 256
OWNERS = 16
CAP = 4
M_ALL = 512
TOKENS = 4096


def draw_w_query(key, part):
    values = jax.random.normal(key, (D, HEADS * HEAD_DIM), jnp.float32)
    values = jnp.clip(values, -6.0, 6.0) * D ** (-0.5)
    return values.astype(jnp.bfloat16)


def level_of(stream_key, dims, pieces, least, largest):
    factor_of, own = 1.0, jax.random.fold_in(stream_key, 6)
    for position, shards_of in pieces:
        draws = jnp.exp(jax.random.uniform(jax.random.fold_in(own, position), (shards_of,), jnp.float32, least / len(pieces), largest / len(pieces)))
        factor_of = factor_of * jnp.repeat(draws, dims[position] // shards_of).reshape([-1 if axis == position else 1 for axis in range(len(dims))])
    return factor_of


def split_up(amount, total, most, lean):
    loads = [(1 << 20) // math.isqrt(rank ** lean) + 1 for rank in range(2, amount + 1)]
    surplus, counts = total - most - (amount - 1), [1] * (amount - 1)
    while surplus > 0:
        free = [i for i in range(amount - 1) if counts[i] < most]
        whole, remaining = sum([loads[i] for i in free]), surplus
        for i in free:
            addition = min(most - counts[i], max(1, remaining * loads[i] // whole), surplus)
            counts[i] = counts[i] + addition
            surplus = surplus - addition
    return np.array([most] + counts)


def ragged_sizes(key, count, total, reach, lean):
    if count == 2:
        one = jax.random.randint(key, (), max(1, total - reach), min(reach, total - 1) + 1)
        return jnp.stack([one, total - one])
    tallies = jnp.asarray(split_up(count, total, reach, lean), jnp.int32)
    twos = (count - 1) // 2
    donor, sink = tallies[1:1 + 2 * twos:2], tallies[2:2 + 2 * twos:2]
    room = jnp.minimum(donor - 1, reach - sink)
    moved = jax.random.randint(jax.random.fold_in(key, 1), (twos,), 0, 1 << 20) % (room + 1)
    tallies = tallies.at[1:1 + 2 * twos:2].set(donor - moved).at[2:2 + 2 * twos:2].set(sink + moved)
    return tallies[jax.random.permutation(jax.random.fold_in(key, 2), count)]


def assign_block(stream_key, own, number, rows, count, top, reach, lean):
    order = jax.random.permutation(stream_key, count)
    crowded, ordinary = portions_of(count, rows * top, reach, lean, True), portions_of(count, rows * top, reach, lean, False)
    places = jnp.arange(count)

    def named(tallies, offset_by):
        used = int((tallies > 0).sum())
        fixed = max(1, used // 4)
        shifted = fixed + (places - fixed + offset_by * (used - fixed)) % max(1, count - fixed)
        return jnp.zeros((count,), jnp.int32).at[order[jnp.where(places < fixed, places, shifted)]].set(jnp.asarray(tallies, jnp.int32))

    tallies = jnp.where(number % 4 == 0, named(crowded, number // 4), named(ordinary, number - number // 4 - 1))
    mixed = jax.random.permutation(jax.random.fold_in(own, 3), count)
    source_of, receiver = mixed[0:count // 2 * 2:2], mixed[1:count // 2 * 2:2]
    room = jnp.minimum(tallies[source_of] - 1, reach - tallies[receiver]) // 2
    room = jnp.where((source_of == order[0]) | (receiver == order[0]) | (tallies[receiver] == 0), 0, jnp.maximum(room, 0))
    shifted = jax.random.randint(jax.random.fold_in(own, 4), (count // 2,), 0, 1 << 20) % (room + 1)
    tallies = tallies.at[source_of].add(-shifted).at[receiver].add(shifted)
    labels = jnp.searchsorted(jnp.cumsum(tallies), jnp.arange(rows * top), side="right").astype(jnp.int32)
    grid = labels.reshape(top, rows).T
    grid = grid[jax.random.permutation(jax.random.fold_in(own, 1), rows)]
    offset_by = jax.random.randint(jax.random.fold_in(own, 2), (rows, 1), 0, top)
    return jnp.take_along_axis(grid, (jnp.arange(top)[None, :] + offset_by) % top, axis=1)


def portions_of(count, total, bound, skew, full):
    portions = [(1 << 20) // math.isqrt(rank ** skew) + 1 for rank in range(1, count + 1)]
    largest = bound if full else min(bound, max(-(-total // count), total * portions[0] // sum(portions)))
    least = 1 if total - largest >= count - 1 else 0
    holding, spare = [largest] + [least] * (count - 1), total - largest - least * (count - 1)
    while spare > 0:
        movable = [i for i in range(1, count) if holding[i] < largest] or [i for i in range(1, count) if holding[i] < bound]
        mass, left = sum([portions[i] for i in movable]), spare
        for i in movable:
            extra = min(bound - holding[i], max(1, left * portions[i] // mass), spare)
            holding[i] = holding[i] + extra
            spare = spare - extra
    return np.array(holding)


def noise(own_key, shape, scale, most, shards=(), kind=jnp.bfloat16):
    level = level_of(own_key, shape, shards, -0.22, 0.18) if shards else 1.0
    values = jax.random.normal(own_key, shape, jnp.float32) * scale * level
    return jnp.minimum(jnp.maximum(values, -most), most).astype(kind)


def setup_inputs(seed: int = 0) -> dict:
    arg_keys = jax.random.split(jax.random.key(seed), 16)
    patch_rows = noise(arg_keys[0], (OWNERS, 4 * M_DEV, VIS_WIDTH), 1.0, 6.0, ((0, 16),))
    ln_gain = jnp.clip(1.0 + 0.1 * jax.random.normal(arg_keys[1], (VIS_WIDTH,), jnp.float32), 0.5, 1.5)
    ln_bias = noise(arg_keys[2], (VIS_WIDTH,), 0.3, 1.5, (), jnp.float32)
    merge_up = noise(arg_keys[3], (4 * VIS_WIDTH, MERGE_HIDDEN), (4 * VIS_WIDTH) ** -0.5, 0.078125, ((1, 64),))
    merge_up_bias = noise(arg_keys[4], (MERGE_HIDDEN,), 0.5, 2.5, ((0, 64),), jnp.float32)
    merge_down = noise(arg_keys[5], (MERGE_HIDDEN, D), MERGE_HIDDEN ** -0.5, 0.078125, ((0, 64),))
    merge_down_bias = noise(arg_keys[6], (D,), 0.5, 2.5, ((0, 64),), jnp.float32)
    row_owner_keys = jax.random.split(jax.random.fold_in(arg_keys[7], 1), M_ALL // M_DEV)
    row_owner_turns = jax.random.permutation(jax.random.fold_in(arg_keys[7], 3), M_ALL // M_DEV)
    row_owner = jax.vmap(lambda own, number: assign_block(jax.random.fold_in(arg_keys[7], 2), own, number, M_DEV, OWNERS, 1, CAP, 2))(row_owner_keys, row_owner_turns).reshape((M_ALL, 1))
    text_embed = noise(arg_keys[8], (OWNERS, S_DEV, D), 1.0, 6.0, ((0, 16),))
    doc_ids = jax.vmap(lambda own: jnp.searchsorted(jnp.cumsum(ragged_sizes(own, 8, S_DEV, S_DEV // 4, 2)), jnp.arange(S_DEV), side="right"))(jax.random.split(arg_keys[9], OWNERS)).reshape((OWNERS, S_DEV)).astype(jnp.int32)
    rms_gain = jnp.clip(1.0 + 0.1 * jax.random.normal(arg_keys[10], (D,), jnp.float32), 0.5, 1.5)
    w_query = draw_w_query(jax.random.fold_in(arg_keys[15], 71), 0)
    query_bias = noise(arg_keys[12], (HEADS * HEAD_DIM,), 0.5, 2.5, ((0, 64),), jnp.float32)
    w_keyval = noise(arg_keys[13], (D, 2, HEAD_DIM * KV_HEADS), D ** -0.5, 0.0625, ((2, 64),))
    keyval_bias = noise(arg_keys[14], (2, HEAD_DIM * KV_HEADS), 0.5, 2.5, ((1, 64),), jnp.float32)
    return dict(patch_rows=patch_rows, ln_gain=ln_gain, ln_bias=ln_bias, merge_up=merge_up, merge_up_bias=merge_up_bias, merge_down=merge_down, merge_down_bias=merge_down_bias, row_owner=row_owner, text_embed=text_embed, doc_ids=doc_ids, rms_gain=rms_gain, w_query=w_query, query_bias=query_bias, w_keyval=w_keyval, keyval_bias=keyval_bias)


def attend_owner(inputs):
    queries, keyval, documents = inputs
    group_size = HEADS // KV_HEADS
    query_f = queries.astype(jnp.float32)
    keys = jnp.repeat(keyval[:, 0], group_size, axis=1).astype(jnp.float32)
    values = jnp.repeat(keyval[:, 1], group_size, axis=1).astype(jnp.float32)
    scores = jnp.einsum('qhd,khd->hqk', query_f, keys) / math.sqrt(HEAD_DIM)
    positions = jnp.arange(S_DEV, dtype=jnp.int32)
    allowed = (documents[:, None] == documents[None, :]) & (positions[None, :] <= positions[:, None])
    scores = jnp.where(allowed[None], scores, jnp.float32(-1e+30))
    highest = lax.optimization_barrier(jnp.max(scores, axis=-1, keepdims=True))
    weights = jnp.exp(scores - highest)
    probs = (weights / lax.optimization_barrier(jnp.sum(weights, axis=-1, keepdims=True))).astype(jnp.bfloat16)
    output = jnp.einsum('hqk,khd->qhd', probs.astype(jnp.float32), values)
    return output.astype(jnp.bfloat16).reshape(S_DEV, HEADS * HEAD_DIM)

def reference(patch_rows, ln_gain, ln_bias, merge_up, merge_up_bias, merge_down, merge_down_bias, row_owner, text_embed, doc_ids, rms_gain, w_query, query_bias, w_keyval, keyval_bias):
    pixels = patch_rows.astype(jnp.float32)
    center = pixels - lax.optimization_barrier(jnp.mean(pixels, axis=-1, keepdims=True))
    spread = lax.optimization_barrier(jnp.mean(center * center, axis=-1, keepdims=True))
    normed_patch = (center * lax.rsqrt(spread + 1e-06) * ln_gain + ln_bias).astype(jnp.bfloat16)
    merged = normed_patch.reshape(OWNERS * M_DEV, 4 * VIS_WIDTH)
    hidden = jax.nn.gelu(jnp.dot(merged, merge_up, preferred_element_type=jnp.float32) + merge_up_bias, approximate=False).astype(jnp.bfloat16)
    vision = (jnp.dot(hidden, merge_down, preferred_element_type=jnp.float32) + merge_down_bias).astype(jnp.bfloat16)
    owner = row_owner[:, 0]
    onehot = (owner[:, None] == jnp.arange(OWNERS, dtype=jnp.int32)[None, :]).astype(jnp.int32)
    ranks = lax.optimization_barrier(jnp.sum((jnp.cumsum(onehot, axis=0) - onehot) * onehot, axis=1)).astype(jnp.int32)
    sequence = text_embed.at[owner, ranks].set(vision)
    seq_f = sequence.astype(jnp.float32)
    normed_seq = (seq_f * lax.rsqrt(lax.optimization_barrier(jnp.mean(seq_f * seq_f, axis=-1, keepdims=True)) + 1e-06) * rms_gain).astype(jnp.bfloat16)
    flat = normed_seq.reshape(TOKENS, D)
    queries = (jnp.dot(flat, w_query, preferred_element_type=jnp.float32) + query_bias).astype(jnp.bfloat16)
    queries = queries.reshape(OWNERS, S_DEV, HEADS, HEAD_DIM)
    keyval = jnp.dot(flat, w_keyval.reshape(D, 2 * KV_HEADS * HEAD_DIM), preferred_element_type=jnp.float32) + keyval_bias.reshape(2 * KV_HEADS * HEAD_DIM)
    keyval = keyval.astype(jnp.bfloat16).reshape(OWNERS, S_DEV, 2, HEAD_DIM, KV_HEADS)
    keyval = jnp.transpose(keyval, (0, 1, 2, 4, 3))
    return lax.map(attend_owner, (queries, keyval, doc_ids))
```

```python
import functools
import math

import jax
import jax.numpy as jnp
from jax import lax
from jax.experimental import pallas as pl
from jax.experimental.pallas import tpu as pltpu
from jax.sharding import PartitionSpec as P

HEADS = 64
KV_HEADS = 8
HEAD_DIM = 128
D = 8192
ROWS = 32
SEQ = 256
NX, NY, NC, NZ = 4, 8, 2, 16
CAP = 4
IMG = NZ * CAP
VIS = 1280
CHUNK = 1024
MESH = pl.DeviceIdType.MESH
BF, F32, I32 = jnp.bfloat16, jnp.float32, jnp.int32

FAR_Y = (4, 3, 5, 2, 6, 1, 7)
NEAR_Y = (1, 7, 2, 6, 3, 5, 4)
FAR_X = (2, 1, 3)
FAR_Z = (8, 7, 9, 6, 10, 5, 11, 4, 12, 3, 13, 2, 14, 1, 15)


def iota(shape, dim):
    return lax.broadcasted_iota(I32, shape, dim)


def onehot(mask):
    return jnp.where(mask, F32(1), F32(0)).astype(BF)


def dot(a, b):
    return jnp.dot(a, b, preferred_element_type=F32)


def dot_nt(a, b):
    return lax.dot_general(a, b, (((1,), (1,)), ((), ())), preferred_element_type=F32)


def kernel(*refs):
    n_in = 15
    ins, out_ref, vin = refs[:n_in], refs[n_in], refs[n_in + 1 : 2 * n_in + 1]
    (ps, cr, xs, xr, os_, ys, yr, zs, zr, gb, k1s, k1, k2, l1s, l1, l2, qt, kvt, sel_s, pls_s, msk_s, merged_s,
     in_sem, snd, cr_sem, xr_sem, yr_sem, zr_sem, gy_sem, gx_sem, gc_sem, k1_sem, k2_sem, l1_sem, l2_sem) = refs[2 * n_in + 1 :]
    (patch, lng, lnb, mut, mub, md, mdb, ro, text, doc, rg, wq, qb, wkv, kvb) = vin

    zhi, zlo, mp = lax.axis_index("group"), lax.axis_index("dp"), lax.axis_index("mp")
    z = zhi * 4 + zlo
    y, x, c = mp // 8, (mp // 2) % 4, mp % 2
    xc = x * 2 + c
    oc = 1 - c

    def at_mp(yy, xx, cc):
        return {"mp": yy * 8 + xx * 2 + cc}

    def at_z(zz):
        return {"group": zz // 4, "dp": zz % 4}

    sibling = at_mp(y, x, oc)
    x_peer = {k: at_mp(y, (x + k) % NX, c) for k in FAR_X}
    y_peer = {k: at_mp((y + k) % NY, x, c) for k in FAR_Y}
    z_peer = {k: at_z((z + k) % NZ) for k in FAR_Z}
    row_peer = {k: at_mp(y, ((xc + k) % 8) // 2, ((xc + k) % 8) % 2) for k in range(1, 8)}

    barrier = pltpu.get_barrier_semaphore()
    others = [sibling] + list(x_peer.values()) + list(y_peer.values()) + list(z_peer.values())
    others += [at_mp(y, (x + k) % NX, oc) for k in FAR_X]
    for peer in others:
        pl.semaphore_signal(barrier, inc=1, device_id=peer, device_id_type=MESH)

    loads = [pltpu.make_async_copy(ins[i], vin[i], in_sem.at[i]) for i in range(n_in)]
    for i in (0, 1, 2, 3, 4, 5, 6, 7, 9, 8, 10, 11, 12, 13, 14):
        loads[i].start()

    sends = []

    def send(src, dst, recv_sem, peer):
        copy = pltpu.make_async_remote_copy(
            src_ref=src, dst_ref=dst, send_sem=snd.at[len(sends)], recv_sem=recv_sem, device_id=peer, device_id_type=MESH
        )
        copy.start()
        sends.append(copy)

    def arrive(ref, sem):
        pltpu.make_async_remote_copy(
            src_ref=ref, dst_ref=ref, send_sem=snd.at[0], recv_sem=sem, device_id=sibling, device_id_type=MESH
        ).wait_recv()

    loads[0].wait()
    order = onehot(iota((128, 128), 1) == (iota((128, 128), 0) % ROWS) * 4 + iota((128, 128), 0) // ROWS)
    pixels = dot(order, patch[...])
    center = pixels - jnp.mean(pixels, axis=-1, keepdims=True)
    spread = jnp.mean(center * center, axis=-1, keepdims=True)
    loads[1].wait()
    loads[2].wait()
    normed = (center * lax.rsqrt(spread + 1e-06) * lng[...][None, :] + lnb[...][None, :]).astype(BF)
    merged_s[...] = normed
    loads[3].wait()
    loads[4].wait()
    up = jnp.zeros((ROWS, 80), F32) + mub[...]
    acc = jnp.zeros((ROWS, 80), F32)
    for p in range(4):
        acc += dot_nt(merged_s[p * ROWS : (p + 1) * ROWS, :], mut[:, p * VIS : (p + 1) * VIS])
    up = acc + up
    hidden = (0.5 * up * (1.0 + lax.erf(up * F32(math.sqrt(0.5))))).astype(BF)
    loads[5].wait()

    def down(i, carry):
        part = dot(hidden, md[:, pl.ds(pl.multiple_of(i * CHUNK, CHUNK), CHUNK)])
        for xx in range(NX):
            for cc in range(NC):
                j = xx * 2 + cc
                ps[cc, xx, i] = part[:, j * 128 : (j + 1) * 128]
        return carry

    lax.fori_loop(0, NY, down, 0)

    pl.semaphore_wait(barrier, len(others))

    for k in FAR_X + (0,):
        slot = (x + k) % NX
        send(ps.at[oc, slot], cr.at[slot], cr_sem.at[slot], sibling)

    loads[7].wait()
    owner = ro[...]
    r_lane = iota((1, 512), 1)
    eq16 = onehot(jnp.broadcast_to(owner, (16, 512)) == iota((16, 512), 0))
    before = onehot((iota((512, 512), 0) < iota((512, 512), 1)) & (iota((512, 512), 0) // ROWS == iota((512, 512), 1) // ROWS))
    earlier = dot(eq16, before)
    block_rank = jnp.sum(earlier * eq16.astype(F32), axis=0, keepdims=True)
    slot_of = owner * 8 + block_rank.astype(I32)
    pick = onehot((jnp.broadcast_to(slot_of, (128, 512)) == iota((128, 512), 0)) & (jnp.broadcast_to(r_lane, (128, 512)) // ROWS == z))
    fold = onehot(iota((512, ROWS), 0) % ROWS == iota((512, ROWS), 1))
    sel_s[...] = dot(pick, fold).astype(BF)
    mine = onehot(jnp.broadcast_to(owner, (16, 512)) == z)
    same = onehot(iota((512, 128), 0) // ROWS == iota((512, 128), 1) // 8)
    ahead = onehot(iota((512, 128), 0) // ROWS < iota((512, 128), 1) // 8)
    count = dot(mine, same)[0:1]
    offset = dot(mine, ahead)[0:1]
    place_k = (iota((1, 128), 1) % 8).astype(F32)
    target = jnp.where(place_k < count, offset + place_k, F32(-1))
    place = jnp.where(jnp.broadcast_to(target, (IMG, 128)) == iota((IMG, 128), 0).astype(F32), F32(1), F32(0))
    pls_s[...] = place.astype(BF)
    msk_s[...] = jnp.broadcast_to(jnp.sum(place, axis=1, keepdims=True), (IMG, 128))

    for k in FAR_X + (0,):
        slot = (x + k) % NX
        arrive(cr.at[slot], cr_sem.at[slot])
        both = ps[c, slot] + cr[slot]
        if k:
            xs[k - 1] = both.astype(BF)
            send(xs.at[k - 1], xr.at[k - 1], xr_sem.at[k - 1], x_peer[k])
        else:
            os_[...] = both

    def project(get):
        def squares(i, total):
            v = get(i).astype(F32)
            v = v * v
            for j in range(CHUNK // 128):
                total = total + v[:, j * 128 : (j + 1) * 128]
            return total

        total = lax.fori_loop(0, D // CHUNK, squares, jnp.zeros((IMG, 128), F32))
        inv = lax.rsqrt(jnp.sum(total, axis=-1, keepdims=True) / D + 1e-06)

        def products(i, carry):
            q, kv = carry
            cols = pl.ds(pl.multiple_of(i * CHUNK, CHUNK), CHUNK)
            n = (get(i).astype(F32) * inv * rg[:, cols]).astype(BF)
            return q + dot(n, wq[cols, :]), kv + dot_nt(n, wkv[:, cols])

        q, kv = lax.fori_loop(0, D // CHUNK, products, (jnp.zeros((IMG, 128), F32), jnp.zeros((IMG, 32), F32)))
        kv_bias = jnp.concatenate([kvb[0:1, :], kvb[1:2, :]], axis=1)
        return (q + qb[...]).astype(BF), (kv + kv_bias).astype(BF)

    def text_rows(r):
        q, kv = project(lambda i: text[r * IMG : (r + 1) * IMG, pl.ds(pl.multiple_of(i * CHUNK, CHUNK), CHUNK)])
        qt[r * IMG : (r + 1) * IMG, :] = q
        kvt[r * IMG : (r + 1) * IMG, :] = kv

    for i in (6, 8, 9, 10, 11, 12, 13, 14):
        loads[i].wait()
    text_rows(0)

    for k in FAR_X:
        arrive(xr.at[k - 1], xr_sem.at[k - 1])
    for k in FAR_Y:
        yy = (y + k) % NY
        tot = os_[yy]
        for j in range(3):
            tot = tot + xr[j, yy].astype(F32)
        ys[k - 1] = tot.astype(BF)
        send(ys.at[k - 1], yr.at[k - 1], yr_sem.at[k - 1], y_peer[k])

    text_rows(1)
    text_rows(2)

    vision = os_[y]
    for j in range(3):
        vision = vision + xr[j, y].astype(F32)
    for k in NEAR_Y:
        arrive(yr.at[k - 1], yr_sem.at[k - 1])
        vision = vision + yr[k - 1].astype(F32)
    vision = (vision + mdb[...]).astype(BF)

    zs[...] = dot(sel_s[...], vision).reshape(NZ, 8, 128).astype(BF)
    for k in FAR_Z:
        send(zs.at[(z + k) % NZ], zr.at[z], zr_sem.at[z], z_peer[k])
    zr[z] = zs[z]

    def pack(kv, halves):
        rows = 4 * halves
        o, i = iota((8 * rows, 32), 0), iota((8 * rows, 32), 1)
        wanted = ((o // 2) % 2) * 16 + (o % 2) * 8 + o // rows
        packed = jnp.zeros((8 * rows, 128), F32)
        for h in range(halves):
            chosen = onehot((i == wanted) & ((o % rows) // 4 == h))
            packed += dot_nt(chosen, kv[h * 128 : (h + 1) * 128, :])
        return packed.reshape(8, rows, 128).astype(BF)

    def head_of(held, h, t):
        rows = held.shape[2]
        r, dd = iota((128, 64 * rows), 1), iota((128, 64 * rows), 0)
        source = ((r // rows) % 8) * 16 + (r // (8 * rows)) * 2 + r % 2
        chosen = onehot((dd == source) & ((r % rows) // 2 == h * 2 + t))
        flat = held[...].astype(F32).reshape(64 * rows, 128).astype(BF)
        return dot(chosen, flat).astype(BF)

    def spread_y(src, dst, sems):
        for k in FAR_Y:
            send(src.at[(y + k) % NY], dst.at[y], sems.at[y], y_peer[k])
        dst[y] = src[y]

    def gather_y(dst, sems):
        for k in NEAR_Y:
            yy = (y + k) % NY
            arrive(dst.at[yy], sems.at[yy])

    def spread_row(src, dst, sems):
        for k in (4, 3, 5, 2, 6, 1, 7):
            send(src, dst.at[xc], sems.at[xc], row_peer[k])
        dst[xc] = src[...]

    def gather_row(dst, sems):
        for k in range(1, 8):
            j = (xc + k) % 8
            arrive(dst.at[j], sems.at[j])

    text_rows(3)
    k1s[...] = pack(kvt[...], 2)
    spread_y(k1s, k1, k1_sem)

    for k in range(1, NZ):
        zz = (z + k) % NZ
        arrive(zr.at[zz], zr_sem.at[zz])
    arrived = zr[...].astype(F32).reshape(NZ * 8, 128).astype(BF)
    placed = dot(pls_s[...], arrived)
    own_text = text[0:IMG, pl.ds(pl.multiple_of(mp * 128, 128), 128)].astype(F32)
    gb[c, x, y] = jnp.where(msk_s[...] > 0.5, placed, own_text).astype(BF)

    def block(xx, k):
        return gb.at[c, xx % NX, (y + k) % NY]

    def share_x(k):
        for kk in (1, 3):
            send(block(x, k), block(x, k), gx_sem.at[x, (y + k) % NY], x_peer[kk])

    def relay_x(j, k):
        frm, to = (3, 1) if j % 2 == 0 else (1, 3)
        src = (x + frm) % NX
        arrive(block(src, k), gx_sem.at[src, (y + k) % NY])
        send(block(src, k), block(src, k), gx_sem.at[src, (y + k) % NY], x_peer[to])

    for k in FAR_Y:
        send(block(x, 0), block(x, 0), gy_sem.at[y], y_peer[k])
    order_y = (0,) + NEAR_Y
    for j, k in enumerate(order_y):
        if k:
            arrive(block(x, k), gy_sem.at[(y + k) % NY])
        share_x(k)
        if j >= 2:
            relay_x(j - 2, order_y[j - 2])
    send(gb.at[c, x], gb.at[c, x], gc_sem.at[x], sibling)
    for j in (6, 7):
        relay_x(j, order_y[j])
    for kk in (1, 3, 2):
        xx = (x + kk) % NX
        for j, k in enumerate(order_y):
            if kk == 2 or j % 2 == (kk == 1):
                continue
            arrive(block(xx, k), gx_sem.at[xx, (y + k) % NY])
        if kk == 2:
            for k in order_y:
                arrive(block(xx, k), gx_sem.at[xx, (y + k) % NY])
        send(gb.at[c, xx], gb.at[c, xx], gc_sem.at[xx], sibling)
    gather_y(k1, k1_sem)
    spread_row(k1, k2, k2_sem)
    for k in (0, 1, 3, 2):
        xx = (x + k) % NX
        arrive(gb.at[oc, xx], gc_sem.at[xx])

    q_late, kv_late = project(
        lambda i: jnp.concatenate([gb[cc, xx, i] for xx in range(NX) for cc in range(NC)], axis=1)
    )
    l1s[...] = pack(jnp.concatenate([kv_late, kvt[IMG:128, :]], axis=0), 1)
    spread_y(l1s, l1, l1_sem)

    docs = doc[...].astype(F32)

    def attend(q, keys, values, q0, k0):
        n, m = q.shape[0], keys.shape[1]
        s = dot(q, keys) / math.sqrt(HEAD_DIM)
        row, col = iota((n, m), 0) + q0, iota((n, m), 1) + k0
        eye = jnp.where(iota((n, n), 0) == iota((n, n), 1), docs[:, q0 : q0 + n], F32(0))
        doc_q = jnp.sum(eye, axis=1, keepdims=True)
        s = jnp.where((doc_q == docs[:, k0 : k0 + m]) & (col <= row), s, F32(-1e30))
        w = jnp.exp(s - jnp.max(s, axis=-1, keepdims=True))
        p = (w / jnp.sum(w, axis=-1, keepdims=True)).astype(BF)
        return dot_nt(p, values).astype(BF)

    gather_row(k2, k2_sem)
    keys = jnp.concatenate([head_of(k2, h, 0) for h in range(2)], axis=1)
    values = jnp.concatenate([head_of(k2, h, 1) for h in range(2)], axis=1)
    out_ref[128:256, :] = attend(qt[128:256, :], keys, values, 128, 0)

    gather_y(l1, l1_sem)
    spread_row(l1, l2, l2_sem)
    gather_row(l2, l2_sem)
    q_first = jnp.concatenate([q_late, qt[IMG:128, :]], axis=0)
    out_ref[0:128, :] = attend(q_first, head_of(l2, 0, 0), head_of(l2, 0, 1), 0, 0)

    for copy in sends:
        copy.wait_send()


def per_device(patch_rows, ln_gain, ln_bias, merge_up, merge_up_bias, merge_down, merge_down_bias, row_owner,
               text_embed, doc_ids, rms_gain, w_query, query_bias, w_keyval, keyval_bias):
    args = (
        patch_rows.reshape(128, VIS),
        ln_gain,
        ln_bias,
        merge_up.T,
        merge_up_bias.reshape(1, 80),
        merge_down,
        merge_down_bias.reshape(1, 128),
        row_owner.reshape(1, 512),
        text_embed.reshape(SEQ, D),
        doc_ids,
        rms_gain.reshape(1, D),
        w_query,
        query_bias.reshape(1, 128),
        jnp.transpose(w_keyval, (1, 2, 0)).reshape(32, D),
        keyval_bias,
    )
    dma = pltpu.SemaphoreType.DMA
    n_sends = 4 + 3 + 7 + 15 + 7 + 7 + 7 + 24 + 4 + 7 + 7
    scratch = [pltpu.VMEM(a.shape, a.dtype) for a in args]
    scratch += [
        pltpu.VMEM((NC, NX, NY, ROWS, 128), F32),
        pltpu.VMEM((NX, NY, ROWS, 128), F32),
        pltpu.VMEM((3, NY, ROWS, 128), BF),
        pltpu.VMEM((3, NY, ROWS, 128), BF),
        pltpu.VMEM((NY, ROWS, 128), F32),
        pltpu.VMEM((7, ROWS, 128), BF),
        pltpu.VMEM((7, ROWS, 128), BF),
        pltpu.VMEM((NZ, 8, 128), BF),
        pltpu.VMEM((NZ, 8, 128), BF),
        pltpu.VMEM((NC, NX, NY, IMG, 128), BF),
        pltpu.VMEM((8, 8, 128), BF),
        pltpu.VMEM((8, 8, 128), BF),
        pltpu.VMEM((8, 8, 8, 128), BF),
        pltpu.VMEM((8, 4, 128), BF),
        pltpu.VMEM((8, 4, 128), BF),
        pltpu.VMEM((8, 8, 4, 128), BF),
        pltpu.VMEM((SEQ, 128), BF),
        pltpu.VMEM((SEQ, 32), BF),
        pltpu.VMEM((128, ROWS), BF),
        pltpu.VMEM((IMG, 128), BF),
        pltpu.VMEM((IMG, 128), F32),
        pltpu.VMEM((128, VIS), BF),
        dma((len(args),)),
        dma((n_sends,)),
        dma((4,)), dma((3,)), dma((7,)), dma((16,)), dma((8,)), dma((4, 8)), dma((4,)),
        dma((8,)), dma((8,)), dma((8,)), dma((8,)),
    ]
    out = pl.pallas_call(
        kernel,
        out_shape=jax.ShapeDtypeStruct((SEQ, 128), BF),
        in_specs=[pl.BlockSpec(memory_space=pl.ANY)] * len(args),
        out_specs=pl.BlockSpec(memory_space=pltpu.VMEM),
        scratch_shapes=scratch,
        compiler_params=pltpu.CompilerParams(
            collective_id=0, has_side_effects=True, vmem_limit_bytes=67043328
        ),
        name="step",
    )(*args)
    return out.reshape(1, SEQ, 128)


def solution(mesh):
    in_specs = (
        P(("group", "dp"), None, None),
        P(None),
        P(None),
        P(None, "mp"),
        P("mp"),
        P("mp", None),
        P("mp"),
        P(None, None),
        P(("group", "dp"), None, None),
        P(("group", "dp"), None),
        P(None),
        P(None, "mp"),
        P("mp"),
        P(None, None, "mp"),
        P(None, "mp"),
    )
    return jax.shard_map(
        per_device,
        mesh=mesh,
        in_specs=in_specs,
        out_specs=P(("group", "dp"), None, "mp"),
        check_vma=False,
    )
```

```python
import functools
import math

import jax
import jax.numpy as jnp
from jax import lax
from jax.experimental import pallas as pl
from jax.experimental.pallas import tpu as pltpu
from jax.sharding import PartitionSpec as P

HEADS = 64
KV_HEADS = 8
HEAD_DIM = 128
D = 8192
ROWS = 32
SEQ = 256
NX, NY, NC, NZ = 4, 8, 2, 16
CAP = 4
IMG = NZ * CAP
VIS = 1280
CHUNK = 1024
MESH = pl.DeviceIdType.MESH
BF, F32, I32 = jnp.bfloat16, jnp.float32, jnp.int32

FAR_Y = (4, 3, 5, 2, 6, 1, 7)
NEAR_Y = (1, 7, 2, 6, 3, 5, 4)
FAR_X = (2, 1, 3)
FAR_Z = (8, 7, 9, 6, 10, 5, 11, 4, 12, 3, 13, 2, 14, 1, 15)


def iota(shape, dim):
    return lax.broadcasted_iota(I32, shape, dim)


def onehot(mask):
    return jnp.where(mask, F32(1), F32(0)).astype(BF)


def dot(a, b):
    return jnp.dot(a, b, preferred_element_type=F32)


def dot_nt(a, b):
    return lax.dot_general(a, b, (((1,), (1,)), ((), ())), preferred_element_type=F32)


def kernel(*refs):
    n_in = 15
    ins, out_ref, vin = refs[:n_in], refs[n_in], refs[n_in + 1 : 2 * n_in + 1]
    (ps, cr, xs, xr, os_, ys, yr, zs, zr, gb, k1s, k1, k2, l1s, l1, l1c, l2, qt, kvt, sel_s, pls_s, msk_s, merged_s,
     in_sem, snd, cr_sem, xr_sem, yr_sem, zr_sem, gy_sem, gx_sem, gc_sem, k1_sem, k2_sem, l1_sem, l2_sem) = refs[2 * n_in + 1 :]
    (patch, lng, lnb, mut, mub, md, mdb, ro, text, doc, rg, wq, qb, wkv, kvb) = vin

    zhi, zlo, mp = lax.axis_index("group"), lax.axis_index("dp"), lax.axis_index("mp")
    z = zhi * 4 + zlo
    y, x, c = mp // 8, (mp // 2) % 4, mp % 2
    xc = x * 2 + c
    oc = 1 - c

    def at_mp(yy, xx, cc):
        return {"mp": yy * 8 + xx * 2 + cc}

    def at_z(zz):
        return {"group": zz // 4, "dp": zz % 4}

    sibling = at_mp(y, x, oc)
    x_peer = {k: at_mp(y, (x + k) % NX, c) for k in FAR_X}
    y_peer = {k: at_mp((y + k) % NY, x, c) for k in FAR_Y}
    z_peer = {k: at_z((z + k) % NZ) for k in FAR_Z}
    row_peer = {k: at_mp(y, ((xc + k) % 8) // 2, ((xc + k) % 8) % 2) for k in range(1, 8)}

    barrier = pltpu.get_barrier_semaphore()
    others = [sibling] + list(x_peer.values()) + list(y_peer.values()) + list(z_peer.values())
    others += [at_mp(y, (x + k) % NX, oc) for k in FAR_X]
    for peer in others:
        pl.semaphore_signal(barrier, inc=1, device_id=peer, device_id_type=MESH)

    loads = [pltpu.make_async_copy(ins[i], vin[i], in_sem.at[i]) for i in range(n_in)]
    for i in (0, 1, 2, 3, 4, 5, 6, 7, 9, 8, 10, 11, 12, 13, 14):
        loads[i].start()

    sends = []

    def send(src, dst, recv_sem, peer):
        copy = pltpu.make_async_remote_copy(
            src_ref=src, dst_ref=dst, send_sem=snd.at[len(sends)], recv_sem=recv_sem, device_id=peer, device_id_type=MESH
        )
        copy.start()
        sends.append(copy)

    def arrive(ref, sem):
        pltpu.make_async_remote_copy(
            src_ref=ref, dst_ref=ref, send_sem=snd.at[0], recv_sem=sem, device_id=sibling, device_id_type=MESH
        ).wait_recv()

    loads[0].wait()
    order = onehot(iota((128, 128), 1) == (iota((128, 128), 0) % ROWS) * 4 + iota((128, 128), 0) // ROWS)
    pixels = dot(order, patch[...])
    center = pixels - jnp.mean(pixels, axis=-1, keepdims=True)
    spread = jnp.mean(center * center, axis=-1, keepdims=True)
    loads[1].wait()
    loads[2].wait()
    normed = (center * lax.rsqrt(spread + 1e-06) * lng[...][None, :] + lnb[...][None, :]).astype(BF)
    merged_s[...] = normed
    loads[3].wait()
    loads[4].wait()
    up = jnp.zeros((ROWS, 80), F32) + mub[...]
    acc = jnp.zeros((ROWS, 80), F32)
    for p in range(4):
        acc += dot_nt(merged_s[p * ROWS : (p + 1) * ROWS, :], mut[:, p * VIS : (p + 1) * VIS])
    up = acc + up
    hidden = (0.5 * up * (1.0 + lax.erf(up * F32(math.sqrt(0.5))))).astype(BF)
    loads[5].wait()

    def down(i, carry):
        part = dot(hidden, md[:, pl.ds(pl.multiple_of(i * CHUNK, CHUNK), CHUNK)])
        for xx in range(NX):
            for cc in range(NC):
                j = xx * 2 + cc
                ps[cc, xx, i] = part[:, j * 128 : (j + 1) * 128]
        return carry

    lax.fori_loop(0, NY, down, 0)

    pl.semaphore_wait(barrier, len(others))

    for k in FAR_X + (0,):
        slot = (x + k) % NX
        send(ps.at[oc, slot], cr.at[slot], cr_sem.at[slot], sibling)

    loads[7].wait()
    owner = ro[...]
    r_lane = iota((1, 512), 1)
    eq16 = onehot(jnp.broadcast_to(owner, (16, 512)) == iota((16, 512), 0))
    before = onehot((iota((512, 512), 0) < iota((512, 512), 1)) & (iota((512, 512), 0) // ROWS == iota((512, 512), 1) // ROWS))
    earlier = dot(eq16, before)
    block_rank = jnp.sum(earlier * eq16.astype(F32), axis=0, keepdims=True)
    slot_of = owner * 8 + block_rank.astype(I32)
    pick = onehot((jnp.broadcast_to(slot_of, (128, 512)) == iota((128, 512), 0)) & (jnp.broadcast_to(r_lane, (128, 512)) // ROWS == z))
    fold = onehot(iota((512, ROWS), 0) % ROWS == iota((512, ROWS), 1))
    sel_s[...] = dot(pick, fold).astype(BF)
    mine = onehot(jnp.broadcast_to(owner, (16, 512)) == z)
    same = onehot(iota((512, 128), 0) // ROWS == iota((512, 128), 1) // 8)
    ahead = onehot(iota((512, 128), 0) // ROWS < iota((512, 128), 1) // 8)
    count = dot(mine, same)[0:1]
    offset = dot(mine, ahead)[0:1]
    place_k = (iota((1, 128), 1) % 8).astype(F32)
    target = jnp.where(place_k < count, offset + place_k, F32(-1))
    place = jnp.where(jnp.broadcast_to(target, (IMG, 128)) == iota((IMG, 128), 0).astype(F32), F32(1), F32(0))
    pls_s[...] = place.astype(BF)
    msk_s[...] = jnp.broadcast_to(jnp.sum(place, axis=1, keepdims=True), (IMG, 128))

    for k in FAR_X + (0,):
        slot = (x + k) % NX
        arrive(cr.at[slot], cr_sem.at[slot])
        both = ps[c, slot] + cr[slot]
        if k:
            xs[k - 1] = both.astype(BF)
            send(xs.at[k - 1], xr.at[k - 1], xr_sem.at[k - 1], x_peer[k])
        else:
            os_[...] = both

    def project(get):
        def squares(i, total):
            v = get(i).astype(F32)
            v = v * v
            for j in range(CHUNK // 128):
                total = total + v[:, j * 128 : (j + 1) * 128]
            return total

        total = lax.fori_loop(0, D // CHUNK, squares, jnp.zeros((IMG, 128), F32))
        inv = lax.rsqrt(jnp.sum(total, axis=-1, keepdims=True) / D + 1e-06)

        def products(i, carry):
            q, kv = carry
            cols = pl.ds(pl.multiple_of(i * CHUNK, CHUNK), CHUNK)
            n = (get(i).astype(F32) * inv * rg[:, cols]).astype(BF)
            return q + dot(n, wq[cols, :]), kv + dot_nt(n, wkv[:, cols])

        q, kv = lax.fori_loop(0, D // CHUNK, products, (jnp.zeros((IMG, 128), F32), jnp.zeros((IMG, 32), F32)))
        kv_bias = jnp.concatenate([kvb[0:1, :], kvb[1:2, :]], axis=1)
        return (q + qb[...]).astype(BF), (kv + kv_bias).astype(BF)

    def text_rows(r):
        q, kv = project(lambda i: text[r * IMG : (r + 1) * IMG, pl.ds(pl.multiple_of(i * CHUNK, CHUNK), CHUNK)])
        qt[r * IMG : (r + 1) * IMG, :] = q
        kvt[r * IMG : (r + 1) * IMG, :] = kv

    for i in (6, 8, 9, 10, 11, 12, 13, 14):
        loads[i].wait()
    text_rows(0)

    for k in FAR_X:
        arrive(xr.at[k - 1], xr_sem.at[k - 1])
    for k in FAR_Y:
        yy = (y + k) % NY
        tot = os_[yy]
        for j in range(3):
            tot = tot + xr[j, yy].astype(F32)
        ys[k - 1] = tot.astype(BF)
        send(ys.at[k - 1], yr.at[k - 1], yr_sem.at[k - 1], y_peer[k])

    text_rows(1)
    text_rows(2)

    vision = os_[y]
    for j in range(3):
        vision = vision + xr[j, y].astype(F32)
    for k in NEAR_Y:
        arrive(yr.at[k - 1], yr_sem.at[k - 1])
        vision = vision + yr[k - 1].astype(F32)
    vision = (vision + mdb[...]).astype(BF)

    zs[...] = dot(sel_s[...], vision).reshape(NZ, 8, 128).astype(BF)
    for k in FAR_Z:
        send(zs.at[(z + k) % NZ], zr.at[z], zr_sem.at[z], z_peer[k])
    zr[z] = zs[z]

    def pack(kv, halves):
        o, i = iota((64, 32), 0), iota((64, 32), 1)
        wanted = ((o // 2) % 2) * 16 + (o % 2) * 8 + o // 8
        packed = jnp.zeros((64, 128), F32)
        for h in range(halves):
            chosen = onehot((i == wanted) & ((o // 4) % 2 == h))
            packed += dot_nt(chosen, kv[h * 128 : (h + 1) * 128, :])
        return packed.reshape(8, 8, 128).astype(BF)

    def flat_of(held):
        return held[...].astype(F32).reshape(-1, 128).astype(BF)

    def head_of(flat, rows, h, t):
        r, dd = iota((128, 64 * rows), 1), iota((128, 64 * rows), 0)
        source = ((r // rows) % 8) * 16 + (r // (8 * rows)) * 2 + r % 2
        chosen = onehot((dd == source) & ((r % rows) // 2 == h * 2 + t))
        return dot(chosen, flat).astype(BF)

    def spread_y(src, dst, sems):
        for k in FAR_Y:
            send(src.at[(y + k) % NY], dst.at[y], sems.at[y], y_peer[k])
        dst[y] = src[y]

    def gather_y(dst, sems):
        for k in NEAR_Y:
            yy = (y + k) % NY
            arrive(dst.at[yy], sems.at[yy])

    def spread_row(src, dst, sems):
        for k in (4, 3, 5, 2, 6, 1, 7):
            send(src, dst.at[xc], sems.at[xc], row_peer[k])
        dst[xc] = src[...]

    def gather_row(dst, sems):
        for k in range(1, 8):
            j = (xc + k) % 8
            arrive(dst.at[j], sems.at[j])

    text_rows(3)
    k1s[...] = pack(kvt[...], 2)
    spread_y(k1s, k1, k1_sem)
    gather_y(k1, k1_sem)
    spread_row(k1, k2, k2_sem)

    for k in range(1, NZ):
        zz = (z + k) % NZ
        arrive(zr.at[zz], zr_sem.at[zz])
    arrived = zr[...].astype(F32).reshape(NZ * 8, 128).astype(BF)
    placed = dot(pls_s[...], arrived)
    own_text = text[0:IMG, pl.ds(pl.multiple_of(mp * 128, 128), 128)].astype(F32)
    gb[c, x, y] = jnp.where(msk_s[...] > 0.5, placed, own_text).astype(BF)

    def block(xx, k):
        return gb.at[c, xx % NX, (y + k) % NY]

    order_y = (0,) + NEAR_Y
    early = order_y[:4]
    for k in FAR_Y:
        send(block(x, 0), block(x, 0), gy_sem.at[y], y_peer[k])
    for k in order_y:
        if k:
            arrive(block(x, k), gy_sem.at[(y + k) % NY])
        for kk in (1, 3) if k in early else FAR_X:
            send(block(x, k), block(x, k), gx_sem.at[x, (y + k) % NY], x_peer[kk])
    nxt = (x + 1) % NX
    for k in early:
        arrive(block(nxt, k), gx_sem.at[nxt, (y + k) % NY])
        send(block(nxt, k), block(nxt, k), gx_sem.at[nxt, (y + k) % NY], x_peer[3])
    send(gb.at[c, x], gb.at[c, x], gc_sem.at[x], sibling)
    for kk in (1, 3, 2):
        xx = (x + kk) % NX
        for k in order_y:
            if kk != 1 or k not in early:
                arrive(block(xx, k), gx_sem.at[xx, (y + k) % NY])
        send(gb.at[c, xx], gb.at[c, xx], gc_sem.at[xx], sibling)
    for k in (0, 1, 3, 2):
        xx = (x + k) % NX
        arrive(gb.at[oc, xx], gc_sem.at[xx])

    q_late, kv_late = project(
        lambda i: jnp.concatenate([gb[cc, xx, i] for xx in range(NX) for cc in range(NC)], axis=1)
    )
    l1s[...] = pack(jnp.concatenate([kv_late, kvt[IMG:128, :]], axis=0), 1)
    spread_y(l1s, l1, l1_sem)

    docs = doc[...].astype(F32)

    def attend(q, keys, values, q0, k0):
        n, m = q.shape[0], keys.shape[1]
        s = dot(q, keys) / math.sqrt(HEAD_DIM)
        row, col = iota((n, m), 0) + q0, iota((n, m), 1) + k0
        eye = jnp.where(iota((n, n), 0) == iota((n, n), 1), docs[:, q0 : q0 + n], F32(0))
        doc_q = jnp.sum(eye, axis=1, keepdims=True)
        s = jnp.where((doc_q == docs[:, k0 : k0 + m]) & (col <= row), s, F32(-1e30))
        w = jnp.exp(s - jnp.max(s, axis=-1, keepdims=True))
        p = (w / jnp.sum(w, axis=-1, keepdims=True)).astype(BF)
        return dot_nt(p, values).astype(BF)

    gather_row(k2, k2_sem)
    flat = flat_of(k2)
    keys = jnp.concatenate([head_of(flat, 8, h, 0) for h in range(2)], axis=1)
    values = jnp.concatenate([head_of(flat, 8, h, 1) for h in range(2)], axis=1)
    out_ref[128:256, :] = attend(qt[128:256, :], keys, values, 128, 0)

    gather_y(l1, l1_sem)
    used = (iota((32, 64), 0) // 4) * 8 + iota((32, 64), 0) % 4
    l1c[...] = dot(onehot(iota((32, 64), 1) == used), flat_of(l1)).reshape(4, 8, 128).astype(BF)
    spread_row(l1c, l2, l2_sem)
    gather_row(l2, l2_sem)
    q_first = jnp.concatenate([q_late, qt[IMG:128, :]], axis=0)
    flat = flat_of(l2)
    out_ref[0:128, :] = attend(q_first, head_of(flat, 4, 0, 0), head_of(flat, 4, 0, 1), 0, 0)

    for copy in sends:
        copy.wait_send()


def per_device(patch_rows, ln_gain, ln_bias, merge_up, merge_up_bias, merge_down, merge_down_bias, row_owner,
               text_embed, doc_ids, rms_gain, w_query, query_bias, w_keyval, keyval_bias):
    args = (
        patch_rows.reshape(128, VIS),
        ln_gain,
        ln_bias,
        merge_up.T,
        merge_up_bias.reshape(1, 80),
        merge_down,
        merge_down_bias.reshape(1, 128),
        row_owner.reshape(1, 512),
        text_embed.reshape(SEQ, D),
        doc_ids,
        rms_gain.reshape(1, D),
        w_query,
        query_bias.reshape(1, 128),
        jnp.transpose(w_keyval, (1, 2, 0)).reshape(32, D),
        keyval_bias,
    )
    dma = pltpu.SemaphoreType.DMA
    n_sends = 4 + 3 + 7 + 15 + 7 + 7 + 7 + 24 + 4 + 7 + 7
    scratch = [pltpu.VMEM(a.shape, a.dtype) for a in args]
    scratch += [
        pltpu.VMEM((NC, NX, NY, ROWS, 128), F32),
        pltpu.VMEM((NX, NY, ROWS, 128), F32),
        pltpu.VMEM((3, NY, ROWS, 128), BF),
        pltpu.VMEM((3, NY, ROWS, 128), BF),
        pltpu.VMEM((NY, ROWS, 128), F32),
        pltpu.VMEM((7, ROWS, 128), BF),
        pltpu.VMEM((7, ROWS, 128), BF),
        pltpu.VMEM((NZ, 8, 128), BF),
        pltpu.VMEM((NZ, 8, 128), BF),
        pltpu.VMEM((NC, NX, NY, IMG, 128), BF),
        pltpu.VMEM((8, 8, 128), BF),
        pltpu.VMEM((8, 8, 128), BF),
        pltpu.VMEM((8, 8, 8, 128), BF),
        pltpu.VMEM((8, 8, 128), BF),
        pltpu.VMEM((8, 8, 128), BF),
        pltpu.VMEM((4, 8, 128), BF),
        pltpu.VMEM((8, 4, 8, 128), BF),
        pltpu.VMEM((SEQ, 128), BF),
        pltpu.VMEM((SEQ, 32), BF),
        pltpu.VMEM((128, ROWS), BF),
        pltpu.VMEM((IMG, 128), BF),
        pltpu.VMEM((IMG, 128), F32),
        pltpu.VMEM((128, VIS), BF),
        dma((len(args),)),
        dma((n_sends,)),
        dma((4,)), dma((3,)), dma((7,)), dma((16,)), dma((8,)), dma((4, 8)), dma((4,)),
        dma((8,)), dma((8,)), dma((8,)), dma((8,)),
    ]
    out = pl.pallas_call(
        kernel,
        out_shape=jax.ShapeDtypeStruct((SEQ, 128), BF),
        in_specs=[pl.BlockSpec(memory_space=pl.ANY)] * len(args),
        out_specs=pl.BlockSpec(memory_space=pltpu.VMEM),
        scratch_shapes=scratch,
        compiler_params=pltpu.CompilerParams(
            collective_id=0, has_side_effects=True, vmem_limit_bytes=67043328
        ),
        name="step",
    )(*args)
    return out.reshape(1, SEQ, 128)


def solution(mesh):
    in_specs = (
        P(("group", "dp"), None, None),
        P(None),
        P(None),
        P(None, "mp"),
        P("mp"),
        P("mp", None),
        P("mp"),
        P(None, None),
        P(("group", "dp"), None, None),
        P(("group", "dp"), None),
        P(None),
        P(None, "mp"),
        P("mp"),
        P(None, None, "mp"),
        P(None, "mp"),
    )
    return jax.shard_map(
        per_device,
        mesh=mesh,
        in_specs=in_specs,
        out_specs=P(("group", "dp"), None, "mp"),
        check_vma=False,
    )
```

```python
import functools
import math

import jax
import jax.numpy as jnp
from jax import lax
from jax.experimental import pallas as pl
from jax.experimental.pallas import tpu as pltpu
from jax.sharding import PartitionSpec as P

HEADS = 64
KV_HEADS = 8
HEAD_DIM = 128
D = 8192
ROWS = 32
SEQ = 256
NX, NY, NC, NZ = 4, 8, 2, 16
CAP = 4
IMG = NZ * CAP
VIS = 1280
CHUNK = 1024
MESH = pl.DeviceIdType.MESH
BF, F32, I32 = jnp.bfloat16, jnp.float32, jnp.int32

FAR_Y = (4, 3, 5, 2, 6, 1, 7)
NEAR_Y = (1, 7, 2, 6, 3, 5, 4)
FAR_X = (2, 1, 3)
FAR_Z = (8, 7, 9, 6, 10, 5, 11, 4, 12, 3, 13, 2, 14, 1, 15)


def iota(shape, dim):
    return lax.broadcasted_iota(I32, shape, dim)


def onehot(mask):
    return jnp.where(mask, F32(1), F32(0)).astype(BF)


def dot(a, b):
    return jnp.dot(a, b, preferred_element_type=F32)


def dot_nt(a, b):
    return lax.dot_general(a, b, (((1,), (1,)), ((), ())), preferred_element_type=F32)


def kernel(*refs):
    n_in = 15
    ins, out_ref, vin = refs[:n_in], refs[n_in], refs[n_in + 1 : 2 * n_in + 1]
    (ps, cr, xs, xr, os_, ys, yr, zs, zr, gb, k1s, k1, k2, l1s, l1, l1c, l2, qt, kvt, sel_s, pls_s, msk_s, merged_s,
     in_sem, snd, cr_sem, xr_sem, yr_sem, zr_sem, gy_sem, gx_sem, gc_sem, k1_sem, k2_sem, l1_sem, l2_sem, near_sem) = refs[2 * n_in + 1 :]
    (patch, lng, lnb, mut, mub, md, mdb, ro, text, doc, rg, wq, qb, wkv, kvb) = vin

    zhi, zlo, mp = lax.axis_index("group"), lax.axis_index("dp"), lax.axis_index("mp")
    z = zhi * 4 + zlo
    y, x, c = mp // 8, (mp // 2) % 4, mp % 2
    xc = x * 2 + c
    oc = 1 - c

    def at_mp(yy, xx, cc):
        return {"mp": yy * 8 + xx * 2 + cc}

    def at_z(zz):
        return {"group": zz // 4, "dp": zz % 4}

    sibling = at_mp(y, x, oc)
    x_peer = {k: at_mp(y, (x + k) % NX, c) for k in FAR_X}
    y_peer = {k: at_mp((y + k) % NY, x, c) for k in FAR_Y}
    z_peer = {k: at_z((z + k) % NZ) for k in FAR_Z}
    row_peer = {k: at_mp(y, ((xc + k) % 8) // 2, ((xc + k) % 8) % 2) for k in range(1, 8)}

    barrier = pltpu.get_barrier_semaphore()
    others = [sibling] + list(x_peer.values()) + list(y_peer.values()) + [z_peer[1], z_peer[15]]
    others += [at_mp(y, (x + k) % NX, oc) for k in FAR_X]
    for peer in others:
        pl.semaphore_signal(barrier, inc=1, device_id=peer, device_id_type=MESH)

    loads = [pltpu.make_async_copy(ins[i], vin[i], in_sem.at[i]) for i in range(n_in)]
    for i in (0, 1, 2, 3, 4, 5, 6, 7, 9, 8, 10, 11, 12, 13, 14):
        loads[i].start()

    sends = []

    def send(src, dst, recv_sem, peer):
        copy = pltpu.make_async_remote_copy(
            src_ref=src, dst_ref=dst, send_sem=snd.at[len(sends)], recv_sem=recv_sem, device_id=peer, device_id_type=MESH
        )
        copy.start()
        sends.append(copy)

    def arrive(ref, sem):
        pltpu.make_async_remote_copy(
            src_ref=ref, dst_ref=ref, send_sem=snd.at[0], recv_sem=sem, device_id=sibling, device_id_type=MESH
        ).wait_recv()

    loads[0].wait()
    order = onehot(iota((128, 128), 1) == (iota((128, 128), 0) % ROWS) * 4 + iota((128, 128), 0) // ROWS)
    pixels = dot(order, patch[...])
    center = pixels - jnp.mean(pixels, axis=-1, keepdims=True)
    spread = jnp.mean(center * center, axis=-1, keepdims=True)
    loads[1].wait()
    loads[2].wait()
    normed = (center * lax.rsqrt(spread + 1e-06) * lng[...][None, :] + lnb[...][None, :]).astype(BF)
    merged_s[...] = normed
    loads[3].wait()
    loads[4].wait()
    up = jnp.zeros((ROWS, 80), F32) + mub[...]
    acc = jnp.zeros((ROWS, 80), F32)
    for p in range(4):
        acc += dot_nt(merged_s[p * ROWS : (p + 1) * ROWS, :], mut[:, p * VIS : (p + 1) * VIS])
    up = acc + up
    hidden = (0.5 * up * (1.0 + lax.erf(up * F32(math.sqrt(0.5))))).astype(BF)
    loads[5].wait()

    def down(i, carry):
        part = dot(hidden, md[:, pl.ds(pl.multiple_of(i * CHUNK, CHUNK), CHUNK)])
        for xx in range(NX):
            for cc in range(NC):
                j = xx * 2 + cc
                ps[cc, xx, i] = part[:, j * 128 : (j + 1) * 128]
        return carry

    lax.fori_loop(0, NY, down, 0, unroll=True)

    pl.semaphore_wait(barrier, len(others))

    def greet(r):
        for k in (1 << r, NZ - (1 << r)):
            pl.semaphore_signal(near_sem.at[r], inc=1, device_id=z_peer[k], device_id_type=MESH)

    def met(r):
        pl.semaphore_wait(near_sem.at[r], 2)

    greet(0)

    for k in FAR_X + (0,):
        slot = (x + k) % NX
        send(ps.at[oc, slot], cr.at[slot], cr_sem.at[slot], sibling)

    met(0)
    greet(1)

    loads[7].wait()
    owner = ro[...]
    r_lane = iota((1, 512), 1)
    eq16 = onehot(jnp.broadcast_to(owner, (16, 512)) == iota((16, 512), 0))
    before = onehot((iota((512, 512), 0) < iota((512, 512), 1)) & (iota((512, 512), 0) // ROWS == iota((512, 512), 1) // ROWS))
    earlier = dot(eq16, before)
    block_rank = jnp.sum(earlier * eq16.astype(F32), axis=0, keepdims=True)
    slot_of = owner * 8 + block_rank.astype(I32)
    pick = onehot((jnp.broadcast_to(slot_of, (128, 512)) == iota((128, 512), 0)) & (jnp.broadcast_to(r_lane, (128, 512)) // ROWS == z))
    fold = onehot(iota((512, ROWS), 0) % ROWS == iota((512, ROWS), 1))
    sel_s[...] = dot(pick, fold).astype(BF)
    mine = onehot(jnp.broadcast_to(owner, (16, 512)) == z)
    same = onehot(iota((512, 128), 0) // ROWS == iota((512, 128), 1) // 8)
    ahead = onehot(iota((512, 128), 0) // ROWS < iota((512, 128), 1) // 8)
    count = dot(mine, same)[0:1]
    offset = dot(mine, ahead)[0:1]
    place_k = (iota((1, 128), 1) % 8).astype(F32)
    target = jnp.where(place_k < count, offset + place_k, F32(-1))
    place = jnp.where(jnp.broadcast_to(target, (IMG, 128)) == iota((IMG, 128), 0).astype(F32), F32(1), F32(0))
    pls_s[...] = place.astype(BF)
    msk_s[...] = jnp.broadcast_to(jnp.sum(place, axis=1, keepdims=True), (IMG, 128))

    for k in FAR_X + (0,):
        slot = (x + k) % NX
        arrive(cr.at[slot], cr_sem.at[slot])
        both = ps[c, slot] + cr[slot]
        if k:
            xs[k - 1] = both.astype(BF)
            send(xs.at[k - 1], xr.at[k - 1], xr_sem.at[k - 1], x_peer[k])
        else:
            os_[...] = both

    def project(get, total=None):
        def squares(i, total):
            v = get(i).astype(F32)
            v = v * v
            for j in range(CHUNK // 128):
                total = total + v[:, j * 128 : (j + 1) * 128]
            return total

        if total is None:
            total = lax.fori_loop(0, D // CHUNK, squares, jnp.zeros((IMG, 128), F32), unroll=True)
        inv = lax.rsqrt(jnp.sum(total, axis=-1, keepdims=True) / D + 1e-06)

        def products(i, carry):
            q, kv = carry
            cols = pl.ds(pl.multiple_of(i * CHUNK, CHUNK), CHUNK)
            n = (get(i).astype(F32) * inv * rg[:, cols]).astype(BF)
            return q + dot(n, wq[cols, :]), kv + dot_nt(n, wkv[:, cols])

        q, kv = lax.fori_loop(0, D // CHUNK, products, (jnp.zeros((IMG, 128), F32), jnp.zeros((IMG, 32), F32)), unroll=True)
        kv_bias = jnp.concatenate([kvb[0:1, :], kvb[1:2, :]], axis=1)
        return (q + qb[...]).astype(BF), (kv + kv_bias).astype(BF)

    def text_rows(r):
        q, kv = project(lambda i: text[r * IMG : (r + 1) * IMG, pl.ds(pl.multiple_of(i * CHUNK, CHUNK), CHUNK)])
        qt[r * IMG : (r + 1) * IMG, :] = q
        kvt[r * IMG : (r + 1) * IMG, :] = kv

    for i in (6, 8, 9, 10, 11, 12, 13, 14):
        loads[i].wait()
    text_rows(0)
    met(1)
    greet(2)

    for k in FAR_X:
        arrive(xr.at[k - 1], xr_sem.at[k - 1])
    for k in FAR_Y:
        yy = (y + k) % NY
        tot = os_[yy]
        for j in range(3):
            tot = tot + xr[j, yy].astype(F32)
        ys[k - 1] = tot.astype(BF)
        send(ys.at[k - 1], yr.at[k - 1], yr_sem.at[k - 1], y_peer[k])

    text_rows(1)
    text_rows(2)

    vision = os_[y]
    for j in range(3):
        vision = vision + xr[j, y].astype(F32)
    for k in NEAR_Y:
        arrive(yr.at[k - 1], yr_sem.at[k - 1])
        vision = vision + yr[k - 1].astype(F32)
    vision = (vision + mdb[...]).astype(BF)

    met(2)

    zs[...] = dot(sel_s[...], vision).reshape(NZ, 8, 128).astype(BF)
    for k in FAR_Z:
        send(zs.at[(z + k) % NZ], zr.at[z], zr_sem.at[z], z_peer[k])
    zr[z] = zs[z]

    def pack(kv, halves):
        o, i = iota((64, 32), 0), iota((64, 32), 1)
        wanted = ((o // 2) % 2) * 16 + (o % 2) * 8 + o // 8
        packed = jnp.zeros((64, 128), F32)
        for h in range(halves):
            chosen = onehot((i == wanted) & ((o // 4) % 2 == h))
            packed += dot_nt(chosen, kv[h * 128 : (h + 1) * 128, :])
        return packed.reshape(8, 8, 128).astype(BF)

    def flat_of(held):
        return held[...].astype(F32).reshape(-1, 128).astype(BF)

    def head_of(flat, rows, h, t):
        r, dd = iota((128, 64 * rows), 1), iota((128, 64 * rows), 0)
        source = ((r // rows) % 8) * 16 + (r // (8 * rows)) * 2 + r % 2
        chosen = onehot((dd == source) & ((r % rows) // 2 == h * 2 + t))
        return dot(chosen, flat).astype(BF)

    def spread_y(src, dst, sems):
        for k in FAR_Y:
            send(src.at[(y + k) % NY], dst.at[y], sems.at[y], y_peer[k])
        dst[y] = src[y]

    def gather_y(dst, sems):
        for k in NEAR_Y:
            yy = (y + k) % NY
            arrive(dst.at[yy], sems.at[yy])

    def spread_row(src, dst, sems):
        for k in (4, 3, 5, 2, 6, 1, 7):
            send(src, dst.at[xc], sems.at[xc], row_peer[k])
        dst[xc] = src[...]

    def gather_row(dst, sems):
        for k in range(1, 8):
            j = (xc + k) % 8
            arrive(dst.at[j], sems.at[j])

    text_rows(3)
    k1s[...] = pack(kvt[...], 2)
    spread_y(k1s, k1, k1_sem)
    gather_y(k1, k1_sem)
    spread_row(k1, k2, k2_sem)

    for k in range(1, NZ):
        zz = (z + k) % NZ
        arrive(zr.at[zz], zr_sem.at[zz])
    arrived = zr[...].astype(F32).reshape(NZ * 8, 128).astype(BF)
    placed = dot(pls_s[...], arrived)
    own_text = text[0:IMG, pl.ds(pl.multiple_of(mp * 128, 128), 128)].astype(F32)
    gb[c, x, y] = jnp.where(msk_s[...] > 0.5, placed, own_text).astype(BF)

    def block(xx, k):
        return gb.at[c, xx % NX, (y + k) % NY]

    order_y = (0,) + NEAR_Y
    early = order_y[:4]
    for k in FAR_Y:
        send(block(x, 0), block(x, 0), gy_sem.at[y], y_peer[k])
    for k in order_y:
        if k:
            arrive(block(x, k), gy_sem.at[(y + k) % NY])
        for kk in (1, 3) if k in early else FAR_X:
            send(block(x, k), block(x, k), gx_sem.at[x, (y + k) % NY], x_peer[kk])
    nxt = (x + 1) % NX
    for k in early:
        arrive(block(nxt, k), gx_sem.at[nxt, (y + k) % NY])
        send(block(nxt, k), block(nxt, k), gx_sem.at[nxt, (y + k) % NY], x_peer[3])
    send(gb.at[c, x], gb.at[c, x], gc_sem.at[x], sibling)

    def squares_of(total, cc, xx):
        for i in range(NY):
            v = gb[cc, xx, i].astype(F32)
            total = total + v * v
        return total

    total = squares_of(jnp.zeros((IMG, 128), F32), c, x)
    for kk in (1, 3, 2):
        xx = (x + kk) % NX
        for k in order_y:
            if kk != 1 or k not in early:
                arrive(block(xx, k), gx_sem.at[xx, (y + k) % NY])
        send(gb.at[c, xx], gb.at[c, xx], gc_sem.at[xx], sibling)
        total = squares_of(total, c, xx)
    for k in (0, 1, 3, 2):
        xx = (x + k) % NX
        arrive(gb.at[oc, xx], gc_sem.at[xx])
        total = squares_of(total, oc, xx)

    q_late, kv_late = project(
        lambda i: jnp.concatenate([gb[cc, xx, i] for xx in range(NX) for cc in range(NC)], axis=1), total
    )
    l1s[...] = pack(jnp.concatenate([kv_late, kvt[IMG:128, :]], axis=0), 1)
    spread_y(l1s, l1, l1_sem)

    docs = doc[...].astype(F32)

    def attend(q, keys, values, q0, k0):
        n, m = q.shape[0], keys.shape[1]
        s = dot(q, keys) / math.sqrt(HEAD_DIM)
        row, col = iota((n, m), 0) + q0, iota((n, m), 1) + k0
        eye = jnp.where(iota((n, n), 0) == iota((n, n), 1), docs[:, q0 : q0 + n], F32(0))
        doc_q = jnp.sum(eye, axis=1, keepdims=True)
        s = jnp.where((doc_q == docs[:, k0 : k0 + m]) & (col <= row), s, F32(-1e30))
        w = jnp.exp(s - jnp.max(s, axis=-1, keepdims=True))
        p = (w / jnp.sum(w, axis=-1, keepdims=True)).astype(BF)
        return dot_nt(p, values).astype(BF)

    gather_row(k2, k2_sem)
    flat = flat_of(k2)
    keys = jnp.concatenate([head_of(flat, 8, h, 0) for h in range(2)], axis=1)
    values = jnp.concatenate([head_of(flat, 8, h, 1) for h in range(2)], axis=1)
    out_ref[128:256, :] = attend(qt[128:256, :], keys, values, 128, 0)

    gather_y(l1, l1_sem)
    used = (iota((32, 64), 0) // 4) * 8 + iota((32, 64), 0) % 4
    l1c[...] = dot(onehot(iota((32, 64), 1) == used), flat_of(l1)).reshape(4, 8, 128).astype(BF)
    spread_row(l1c, l2, l2_sem)
    gather_row(l2, l2_sem)
    q_first = jnp.concatenate([q_late, qt[IMG:128, :]], axis=0)
    flat = flat_of(l2)
    out_ref[0:128, :] = attend(q_first, head_of(flat, 4, 0, 0), head_of(flat, 4, 0, 1), 0, 0)

    for copy in sends:
        copy.wait_send()


def per_device(patch_rows, ln_gain, ln_bias, merge_up, merge_up_bias, merge_down, merge_down_bias, row_owner,
               text_embed, doc_ids, rms_gain, w_query, query_bias, w_keyval, keyval_bias):
    args = (
        patch_rows.reshape(128, VIS),
        ln_gain,
        ln_bias,
        merge_up.T,
        merge_up_bias.reshape(1, 80),
        merge_down,
        merge_down_bias.reshape(1, 128),
        row_owner.reshape(1, 512),
        text_embed.reshape(SEQ, D),
        doc_ids,
        rms_gain.reshape(1, D),
        w_query,
        query_bias.reshape(1, 128),
        jnp.transpose(w_keyval, (1, 2, 0)).reshape(32, D),
        keyval_bias,
    )
    dma = pltpu.SemaphoreType.DMA
    n_sends = 4 + 3 + 7 + 15 + 7 + 7 + 7 + 24 + 4 + 7 + 7
    scratch = [pltpu.VMEM(a.shape, a.dtype) for a in args]
    scratch += [
        pltpu.VMEM((NC, NX, NY, ROWS, 128), F32),
        pltpu.VMEM((NX, NY, ROWS, 128), F32),
        pltpu.VMEM((3, NY, ROWS, 128), BF),
        pltpu.VMEM((3, NY, ROWS, 128), BF),
        pltpu.VMEM((NY, ROWS, 128), F32),
        pltpu.VMEM((7, ROWS, 128), BF),
        pltpu.VMEM((7, ROWS, 128), BF),
        pltpu.VMEM((NZ, 8, 128), BF),
        pltpu.VMEM((NZ, 8, 128), BF),
        pltpu.VMEM((NC, NX, NY, IMG, 128), BF),
        pltpu.VMEM((8, 8, 128), BF),
        pltpu.VMEM((8, 8, 128), BF),
        pltpu.VMEM((8, 8, 8, 128), BF),
        pltpu.VMEM((8, 8, 128), BF),
        pltpu.VMEM((8, 8, 128), BF),
        pltpu.VMEM((4, 8, 128), BF),
        pltpu.VMEM((8, 4, 8, 128), BF),
        pltpu.VMEM((SEQ, 128), BF),
        pltpu.VMEM((SEQ, 32), BF),
        pltpu.VMEM((128, ROWS), BF),
        pltpu.VMEM((IMG, 128), BF),
        pltpu.VMEM((IMG, 128), F32),
        pltpu.VMEM((128, VIS), BF),
        dma((len(args),)),
        dma((n_sends,)),
        dma((4,)), dma((3,)), dma((7,)), dma((16,)), dma((8,)), dma((4, 8)), dma((4,)),
        dma((8,)), dma((8,)), dma((8,)), dma((8,)),
        pltpu.SemaphoreType.REGULAR((3,)),
    ]
    out = pl.pallas_call(
        kernel,
        out_shape=jax.ShapeDtypeStruct((SEQ, 128), BF),
        in_specs=[pl.BlockSpec(memory_space=pl.ANY)] * len(args),
        out_specs=pl.BlockSpec(memory_space=pltpu.VMEM),
        scratch_shapes=scratch,
        compiler_params=pltpu.CompilerParams(
            collective_id=0, has_side_effects=True, vmem_limit_bytes=67043328
        ),
        name="step",
    )(*args)
    return out.reshape(1, SEQ, 128)


def solution(mesh):
    in_specs = (
        P(("group", "dp"), None, None),
        P(None),
        P(None),
        P(None, "mp"),
        P("mp"),
        P("mp", None),
        P("mp"),
        P(None, None),
        P(("group", "dp"), None, None),
        P(("group", "dp"), None),
        P(None),
        P(None, "mp"),
        P("mp"),
        P(None, None, "mp"),
        P(None, "mp"),
    )
    return jax.shard_map(
        per_device,
        mesh=mesh,
        in_specs=in_specs,
        out_specs=P(("group", "dp"), None, "mp"),
        check_vma=False,
    )
```
